512 devices in a mesh: dp: 16 (over z), tensor: 32 (over y, x, core).
Axes of the slice: x: 4, y: 4, z: 16, core: 2. Of those that a mesh axis runs over, the one named last changes fastest.
Arguments:
- acts: bfloat16 [16, 512, 4096], P('dp', None, 'tensor'), may hold values from -6 to 6
- grads: bfloat16 [16, 512, 4096], P('dp', None, 'tensor'), may hold values from -6 to 6
- basis_in_held: bfloat16 [16, 4096, 4096], P('dp', None, 'tensor'), may hold values from -0.09375 to 0.09375
- basis_out_held: bfloat16 [16, 4096, 4096], P('dp', None, 'tensor'), may hold values from -0.09375 to 0.09375
- owners: int32 [2, 32], replicated, may hold values from 0 to 15
- eig_lambda: bfloat16 [4096, 4096], P('tensor'), may hold values from 0.0049743652 to 0.19921875
Outputs:
- precond: bfloat16 [16, 4096, 4096], P('dp', 'tensor')
The draws below stay inside these ranges and needn't reach their ends.
Inputs may be any that keep to these rules, and one draw needn't show every extreme that they name: `owners`: row 0 is for the input eigenbasis, row 1 for the output eigenbasis; entry j names the dp group whose copy of column block j is current, the other copies of that block are stale.
All inputs are finite; a program needn't handle non-finite values.
Results may differ from the reference program's by a relative error of at most 0.0057.
Values may be sent and summed in bfloat16 or wider, within the bound.
A program may use at most 64 MiB of HBM per device.

```python
import math
import jax
import jax.numpy as jnp
from jax import lax

D = 4096
TOK = 512
EXAMPLES = 16
N_DP = 16
N_TENSOR = 32


def with_ends(array, key, smallest, top_value):
    longest = array.shape.index(max(array.shape))
    spots = []
    for shift in (0, 1):
        where = [jax.random.randint(jax.random.fold_in(key, axis), (), 0, length) for axis, length in enumerate(array.shape)]
        where[longest] = (where[longest] + shift) % array.shape[longest]
        spots.append(tuple(where))
    return array.at[spots[0]].set(smallest).at[spots[1]].set(top_value)


def block_scale(own_key, shape, shards, smallest, largest):
    loudness = 1.0
    for axis_at, shards_of in shards:
        heights = jax.random.uniform(jax.random.fold_in(jax.random.fold_in(own_key, 6), axis_at), (shards_of,), jnp.float32, smallest / len(shards), largest / len(shards))
        loudness = loudness * jnp.repeat(jnp.exp(heights), shape[axis_at] // shards_of).reshape((-1,) + (1,) * (len(shape) - 1 - axis_at))
    return loudness


def scatter_about(own_key, shape, spread, most, cuts=(), kind=jnp.bfloat16):
    entries = spread * jax.random.normal(own_key, shape, jnp.float32)
    if cuts:
        entries = entries * block_scale(own_key, shape, cuts, -0.22, 0.18)
    return jnp.clip(entries, -most, most).astype(kind)


def setup_inputs(seed: int = 0) -> dict:
    streams_of = jax.random.split(jax.random.key(seed), 7)
    acts = scatter_about(streams_of[0], (EXAMPLES, TOK, D), 1.0, 6.0, ((0, 16), (2, 32)))
    grads = scatter_about(streams_of[1], (EXAMPLES, TOK, D), 1.0, 6.0, ((0, 16), (2, 32)))
    basis_in_held = scatter_about(streams_of[2], (EXAMPLES, D, D), D ** -0.5, 0.09375, ((0, 16), (2, 32)))
    basis_out_held = scatter_about(streams_of[3], (EXAMPLES, D, D), D ** -0.5, 0.09375, ((0, 16), (2, 32)))
    owners = with_ends(jax.random.randint(streams_of[4], (2, N_TENSOR), 0, N_DP), jax.random.fold_in(streams_of[4], 1), 0, N_DP - 1).astype(jnp.int32)
    eig_lambda = jnp.clip(jnp.exp(math.log(0.19921875) - 3.6901057 * jax.random.uniform(streams_of[5], (D, D), jnp.float32) ** block_scale(streams_of[5], (D, D), ((0, 32),), -0.2, 0.2)), 0.0049743652, 0.19921875).astype(jnp.bfloat16)
    return {"acts": acts, "grads": grads, "basis_in_held": basis_in_held, "basis_out_held": basis_out_held, "owners": owners, "eig_lambda": eig_lambda}


damping = 0.01


def assemble(held, picks):
    width = D // N_TENSOR
    blocks = held.reshape(N_DP, D, N_TENSOR, width)
    chosen = blocks[picks, :, jnp.arange(N_TENSOR, dtype=jnp.int32), :]
    return jnp.transpose(chosen, (1, 0, 2)).reshape(D, D)


def reference(acts, grads, basis_in_held, basis_out_held, owners, eig_lambda):
    basis_in = assemble(basis_in_held, owners[0])
    basis_out = assemble(basis_out_held, owners[1])
    denom = eig_lambda.astype(jnp.float32) + damping

    def one_example(pair):
        inputs, outputs = pair
        rot_in = jnp.dot(inputs, basis_in, preferred_element_type=jnp.float32).astype(jnp.bfloat16)
        rot_out = jnp.dot(outputs, basis_out, preferred_element_type=jnp.float32).astype(jnp.bfloat16)
        product = jnp.dot(rot_out.T, rot_in, preferred_element_type=jnp.float32) / TOK
        return (product / denom).astype(jnp.bfloat16)

    return lax.map(one_example, (acts, grads))
```

```python
import functools

import jax
import jax.numpy as jnp
from jax import lax
from jax.experimental import pallas as pl
from jax.experimental.pallas import tpu as pltpu
from jax.sharding import PartitionSpec as P

damping = 0.01
MESH = pl.DeviceIdType.MESH
NX = 4
NY = 4
SUBS = 2
ALL = slice(None)


class Slots:
    def __init__(self, sems):
        self.sems = sems
        self.used = 0

    def take(self):
        self.used += 1
        return self.sems.at[self.used - 1]


class Plane:
    def __init__(self, buf, where, to, send, recv):
        self.buf, self.to, self.send, self.recv = buf, to, send, recv
        self.y, self.x, self.c = where
        self.landing = {}
        self.sent = []
        self.partner = []

    def at(self, dx, dy, part, core=None):
        y = lax.rem(self.y + (dy % NY), NY)
        x = lax.rem(self.x + (dx % NX), NX)
        return self.buf.at[(y, x, self.c if core is None else core) + part]

    def push(self, way, dx, dy, part):
        wx, wy = {"+x": (1, 0), "-x": (-1, 0), "+y": (0, 1), "-y": (0, -1)}[way]
        region = self.at(dx, dy, part)
        recv = self.recv.take()
        copy = pltpu.make_async_remote_copy(
            region, region, self.send.take(), recv, device_id=self.to[way], device_id_type=MESH
        )
        copy.start()
        self.sent.append(copy)
        lands = self.at(dx - wx, dy - wy, part)
        self.landing[(way, (dx - wx) % NX, (dy - wy) % NY, str(part))] = pltpu.make_async_remote_copy(
            lands, lands, self.send.sems.at[0], recv, device_id=self.to[way], device_id_type=MESH
        )

    def arrive(self, way, dx, dy, part):
        self.landing.pop((way, dx % NX, dy % NY, str(part))).wait_recv()

    def share(self, dx, dy):
        region = self.at(dx, dy, ())
        recv = self.recv.take()
        copy = pltpu.make_async_remote_copy(
            region, region, self.send.take(), recv, device_id=self.to["core"], device_id_type=MESH
        )
        copy.start()
        self.sent.append(copy)
        lands = self.at(dx, dy, (), 1 - self.c)
        self.partner.append(
            pltpu.make_async_remote_copy(
                lands, lands, self.send.sems.at[0], recv, device_id=self.to["core"], device_id_type=MESH
            )
        )

    def waves(self):
        return [self.wave1, self.wave2, self.wave3, self.wave4, self.wave5, self.wave6]

    def wave1(self):
        for way in ("+x", "-x", "+y", "-y"):
            self.push(way, 0, 0, ())
        self.share(0, 0)

    def wave2(self):
        top, bottom = (ALL, 0), (ALL, 1)
        for way, dx, dy, part, half, across in (
            ("+x", -1, 0, top, (0,), ("+y", "-y")),
            ("-x", 1, 0, bottom, (0,), ("+y", "-y")),
            ("+y", 0, -1, top, (1,), ("+x", "-x")),
            ("-y", 0, 1, bottom, (1,), ("+x", "-x")),
        ):
            self.arrive(way, dx, dy, ())
            self.push(way, dx, dy, part)
            for side in across:
                self.push(side, dx, dy, half)
            self.share(dx, dy)

    def wave3(self):
        top, bottom = (ALL, 0), (ALL, 1)
        self.arrive("+x", 2, 0, top)
        self.arrive("-x", 2, 0, bottom)
        self.push("+y", 2, 0, (0,))
        self.push("-y", 2, 0, (0,))
        self.arrive("+y", 0, 2, top)
        self.arrive("-y", 0, 2, bottom)
        self.push("+x", 0, 2, (1,))
        self.push("-x", 0, 2, (1,))
        for way, dx, dy, part, on in (
            ("+y", -1, -1, (0,), (0, 0)),
            ("+y", 1, -1, (0,), (0, 0)),
            ("-y", -1, 1, (0,), (0, 1)),
            ("-y", 1, 1, (0,), (0, 1)),
            ("+x", -1, -1, (1,), (1, 0)),
            ("+x", -1, 1, (1,), (1, 0)),
            ("-x", 1, -1, (1,), (1, 1)),
            ("-x", 1, 1, (1,), (1, 1)),
        ):
            self.arrive(way, dx, dy, part)
            self.push(way, dx, dy, on)
        for dx, dy in ((2, 0), (0, 2), (-1, -1), (1, -1), (-1, 1), (1, 1)):
            self.share(dx, dy)

    def wave4(self):
        for way, dx, dy, part, on in (
            ("+y", 2, -1, (0,), (0, 0)),
            ("-y", 2, 1, (0,), (0, 1)),
            ("+x", -1, 2, (1,), (1, 0)),
            ("-x", 1, 2, (1,), (1, 1)),
        ):
            self.arrive(way, dx, dy, part)
            self.push(way, dx, dy, on)
        for far in (-1, 1):
            self.arrive("+y", far, 2, (0, 0))
            self.arrive("-y", far, 2, (0, 1))
            self.arrive("+x", 2, far, (1, 0))
            self.arrive("-x", 2, far, (1, 1))
        for dx, dy in ((-1, 2), (1, 2), (2, -1), (2, 1)):
            self.share(dx, dy)

    def wave5(self):
        self.arrive("+y", 2, 2, (0, 0))
        self.arrive("-y", 2, 2, (0, 1))
        self.arrive("+x", 2, 2, (1, 0))
        self.arrive("-x", 2, 2, (1, 1))
        self.share(2, 2)
        assert not self.landing

    def wave6(self):
        for copy in self.partner:
            copy.wait_recv()

    def drain(self):
        for copy in self.sent:
            copy.wait_send()


class Ring:
    def __init__(self, n, z, held, full, got, owner, up, down, send, recv, landed):
        self.n, self.z, self.held, self.full, self.got = n, z, held, full, got
        self.owner, self.to = owner, (up, down)
        self.hops = (n // 2, n // 2 - 1)
        self.landed = landed
        self.recv = [[[recv.take() for _ in range(SUBS)] for _ in range(2 * h)] for h in self.hops]
        self.send = [[send.take() for _ in range(SUBS)] for _ in range(2)]
        self.flying = {}

    def wrap(self, p):
        return lax.rem(p + 4 * self.n, self.n)

    def go(self, side, step, sub, src, dst):
        if (side, sub) in self.flying:
            self.flying.pop((side, sub)).wait_send()
        copy = pltpu.make_async_remote_copy(
            src,
            dst,
            self.send[side][sub],
            self.recv[side][step][sub],
            device_id=self.to[side],
            device_id_type=MESH,
        )
        copy.start()
        self.flying[(side, sub)] = copy

    def came(self, side, step, sub, where):
        pltpu.make_async_remote_copy(
            where,
            where,
            self.send[side][sub],
            self.recv[side][step][sub],
            device_id=self.to[side],
            device_id_type=MESH,
        ).wait_recv()

    def slot(self, side, step, sub):
        return self.got.at[side * self.hops[0] + step, sub]

    def piece_out(self, side, step):
        h = self.hops[side]
        return self.wrap(self.z + h - step if side == 0 else self.z - h + step)

    def step(self, k):
        h0 = self.hops[0]
        mine = self.owner == self.z
        for sub in range(SUBS):
            for side in (0, 1):
                h = self.hops[side]
                if k < h:
                    src = self.held.at[self.piece_out(side, k), sub]
                    if k > 0:
                        slot = self.slot(side, k - 1, sub)
                        self.came(side, k - 1, sub, slot)
                        slot[...] = jnp.where(mine, src[...], slot[...])
                        src = slot
                    self.go(side, k, sub, src, self.slot(side, k, sub))
                elif k < h0:
                    self.came(side, k - 1, sub, self.slot(side, k - 1, sub))
            if k == h0:
                self.came(0, k - 1, sub, self.slot(0, k - 1, sub))
                if self.hops[1] == h0:
                    self.came(1, k - 1, sub, self.slot(1, k - 1, sub))
                back = self.z - self.owner
                back = jnp.where(back < 0, back + self.n, back)
                here = self.full.at[self.z, sub]
                above = self.slot(1, self.hops[1] - 1, sub)[...]
                below = self.slot(0, h0 - 1, sub)[...]
                other = jnp.where(back <= h0, below, above)
                here[...] = jnp.where(mine, self.held[self.z, sub], other)
                for side in (0, 1):
                    self.go(side, self.hops[side], sub, here, here)
            if k > h0:
                for side in (0, 1):
                    h = self.hops[side]
                    j = k - h0 - 1
                    if j >= h:
                        continue
                    p = self.came_piece(side, j)
                    block = self.full.at[p, sub]
                    self.came(side, h + j, sub, block)
                    if j + 1 < h:
                        self.go(side, h + j + 1, sub, block, block)
        if k == h0:
            self.landed(self.z)
        if k > h0:
            for side in (0, 1):
                j = k - h0 - 1
                if j < self.hops[side]:
                    self.landed(self.came_piece(side, j))

    def came_piece(self, side, j):
        return self.wrap(self.z - 1 - j if side == 0 else self.z + 1 + j)

    def steps(self):
        return 2 * self.hops[0] + 1

    def drain(self):
        for copy in self.flying.values():
            copy.wait_send()


def body(
    n_dp,
    owners,
    acts,
    grads,
    held_in_hbm,
    held_out_hbm,
    eig_hbm,
    out_hbm,
    all_acts,
    all_grads,
    all_rot,
    held_in,
    held_out,
    full_in,
    full_out,
    got_in,
    got_out,
    sum_in,
    sum_out,
    eig,
    out,
    send_sems,
    recv_sems,
    load_sems,
):
    z = lax.axis_index("dp")
    t = lax.axis_index("tensor")
    c = lax.rem(t, 2)
    x = lax.rem(lax.div(t, 2), NX)
    y = lax.div(t, 2 * NX)

    def chip(yy, xx, cc):
        return (z, (lax.rem(yy + NY, NY) * NX + lax.rem(xx + NX, NX)) * 2 + cc)

    to = {
        "+x": chip(y, x + 1, c),
        "-x": chip(y, x - 1, c),
        "+y": chip(y + 1, x, c),
        "-y": chip(y - 1, x, c),
        "core": chip(y, x, 1 - c),
    }
    up = (lax.rem(z + 1, n_dp), t)
    down = (lax.rem(z + n_dp - 1, n_dp), t)

    loads = [
        pltpu.make_async_copy(held_in_hbm, held_in, load_sems.at[0]),
        pltpu.make_async_copy(acts, all_acts.at[y, x, c], load_sems.at[1]),
        pltpu.make_async_copy(held_out_hbm, held_out, load_sems.at[2]),
        pltpu.make_async_copy(grads, all_grads.at[y, x, c], load_sems.at[3]),
        pltpu.make_async_copy(eig_hbm, eig, load_sems.at[4]),
    ]
    for load in loads:
        load.start()

    barrier = pltpu.get_barrier_semaphore()
    around = list(to.values()) + [up, down]
    for device in around:
        pl.semaphore_signal(barrier, inc=1, device_id=device, device_id_type=MESH)
    pl.semaphore_wait(barrier, len(around))

    send, recv = Slots(send_sems), Slots(recv_sems)
    acts_plane = Plane(all_acts, (y, x, c), to, send, recv)
    grads_plane = Plane(all_grads, (y, x, c), to, send, recv)
    rot_plane = Plane(all_rot, (y, x, c), to, send, recv)
    chunk = lambda ref, p, core: ref[lax.div(p, NX), lax.rem(p, NX), core].reshape(-1, ref.shape[-1])

    def add_to(total, ref, full):
        def landed(p):
            left = jnp.concatenate([chunk(ref, p, 0), chunk(ref, p, 1)], axis=1)
            right = full[p].reshape(-1, full.shape[-1])
            total[...] += jnp.dot(left, right, preferred_element_type=jnp.float32)

        return landed

    ring_in = Ring(
        n_dp, z, held_in, full_in, got_in, owners[0, t], up, down, send, recv, add_to(sum_in, all_acts, full_in)
    )
    ring_out = Ring(
        n_dp, z, held_out, full_out, got_out, owners[1, t], up, down, send, recv, add_to(sum_out, all_grads, full_out)
    )
    sum_in[...] = jnp.zeros_like(sum_in)
    sum_out[...] = jnp.zeros_like(sum_out)

    aw, gw, rw = acts_plane.waves(), grads_plane.waves(), rot_plane.waves()
    extra = {0: [1], 2: [2], 4: [3], 6: [4], 7: [5, 6]}
    extra_g = {3: [1], 6: [2], 9: [3], 12: [4], 14: [5, 6]}
    loads[0].wait()
    loads[1].wait()
    for k in range(ring_in.steps()):
        if k == 1:
            loads[2].wait()
        if k == 3:
            loads[3].wait()
        ring_in.step(k)
        if k % 2 == 1:
            ring_out.step(k // 2)
        for w in extra.get(k, ()):
            aw[w - 1]()
        for w in extra_g.get(k, ()):
            gw[w - 1]()

    rot = sum_in[...].astype(jnp.bfloat16)
    all_rot.at[y, x, c][...] = rot.reshape(all_rot.shape[3:])
    rw[0]()
    k = 8
    for w in (1, 2, 3, 4, 5):
        for _ in range(2):
            if k < ring_out.steps():
                ring_out.step(k)
                k += 1
        if w < 5:
            rw[w]()
    loads[4].wait()

    turned = jnp.transpose(sum_out[...]).astype(jnp.bfloat16)
    rw[5]()
    tokens = float(sum_in.shape[0])
    for p in range(NX * NY):
        right = jnp.concatenate([chunk(all_rot, p, 0), chunk(all_rot, p, 1)], axis=1)
        product = jnp.dot(turned, right, preferred_element_type=jnp.float32) / tokens
        cols = pl.ds(p * right.shape[1], right.shape[1])
        out[:, cols] = (product / (eig[:, cols].astype(jnp.float32) + damping)).astype(jnp.bfloat16)
    store = pltpu.make_async_copy(out, out_hbm, load_sems.at[5])
    store.start()
    for user in (acts_plane, grads_plane, rot_plane, ring_in, ring_out):
        user.drain()
    store.wait()


def shards(n_dp, acts, grads, basis_in_held, basis_out_held, owners, eig_lambda):
    tok, width = acts.shape[1:]
    depth = basis_in_held.shape[1]
    rows = depth // n_dp // SUBS
    slice_shape = (2, 2, tok // 4, width)
    held_shape = (n_dp, SUBS, rows, width)
    any_space = pl.BlockSpec(memory_space=pl.ANY)
    bf16, f32 = jnp.bfloat16, jnp.float32
    out = pl.pallas_call(
        functools.partial(body, n_dp),
        out_shape=jax.ShapeDtypeStruct(eig_lambda.shape, bf16),
        in_specs=[pl.BlockSpec(memory_space=pltpu.SMEM)] + [any_space] * 5,
        out_specs=any_space,
        scratch_shapes=[
            pltpu.VMEM((NY, NX, 2) + slice_shape, bf16),
            pltpu.VMEM((NY, NX, 2) + slice_shape, bf16),
            pltpu.VMEM((NY, NX, 2) + slice_shape, bf16),
            pltpu.VMEM(held_shape, bf16),
            pltpu.VMEM(held_shape, bf16),
            pltpu.VMEM(held_shape, bf16),
            pltpu.VMEM(held_shape, bf16),
            pltpu.VMEM((n_dp - 1,) + held_shape[1:], bf16),
            pltpu.VMEM((n_dp - 1,) + held_shape[1:], bf16),
            pltpu.VMEM((tok, width), f32),
            pltpu.VMEM((tok, width), f32),
            pltpu.VMEM(eig_lambda.shape, bf16),
            pltpu.VMEM(eig_lambda.shape, bf16),
            pltpu.SemaphoreType.DMA((152,)),
            pltpu.SemaphoreType.DMA((144 + 4 * (n_dp - 1) * SUBS,)),
            pltpu.SemaphoreType.DMA((6,)),
        ],
        compiler_params=pltpu.CompilerParams(
            collective_id=0, has_side_effects=True, vmem_limit_bytes=56 * 1024 * 1024
        ),
    )(
        owners,
        acts[0].reshape(slice_shape),
        grads[0].reshape(slice_shape),
        basis_in_held[0].reshape(held_shape),
        basis_out_held[0].reshape(held_shape),
        eig_lambda,
    )
    return out[None]


def solution(mesh):
    placed = (
        P("dp", None, "tensor"),
        P("dp", None, "tensor"),
        P("dp", None, "tensor"),
        P("dp", None, "tensor"),
        P(),
        P("tensor", None),
    )
    return jax.shard_map(
        functools.partial(shards, mesh.shape["dp"]),
        mesh=mesh,
        in_specs=placed,
        out_specs=P("dp", "tensor", None),
        check_vma=False,
    )
```

```python
import functools

import jax
import jax.numpy as jnp
from jax import lax
from jax.experimental import pallas as pl
from jax.experimental.pallas import tpu as pltpu
from jax.sharding import PartitionSpec as P

damping = 0.01
MESH = pl.DeviceIdType.MESH
NX = 4
NY = 4
SUBS = 2
ORDER = (
    "i0 o0 a1 e0", "i1 o1 i2 o2", "a2 i3 o3 i4", "o4 a3 i5 o5", "a4 i6 o6 a5", "a6 g1 i7 o7",
    "i8 o8 g2 i9", "o9 i10 o10 g3", "i11 o11 g4 i12", "o12 r1 g5 g6", "o13 r2 o14 r3", "o15 r4 o16 t0",
    "r5",
)


class Slots:
    def __init__(self, sems):
        self.sems = sems
        self.used = 0

    def take(self):
        self.used += 1
        return self.sems.at[self.used - 1]


class Plane:
    WAYS = {"x2": (2, 0), "+x": (1, 0), "-x": (-1, 0), "y2": (0, 2), "+y": (0, 1), "-y": (0, -1)}
    NEAR = ((-1, 0), (1, 0), (0, -1), (0, 1))
    AXES = ((2, 0), (0, 2))
    CORNERS = ((-1, -1), (1, -1), (-1, 1), (1, 1), (-1, 2), (1, 2), (2, -1), (2, 1), (2, 2))

    def __init__(self, buf, where, to, send, recv):
        self.buf, self.to, self.send, self.recv = buf, to, send, recv
        self.y, self.x, self.c = where
        self.landing = {}
        self.partner = {}
        self.sent = []

    def chip(self, dx, dy):
        return lax.rem(self.y + (dy % NY), NY), lax.rem(self.x + (dx % NX), NX)

    def move(self, way, region, lands):
        recv = self.recv.take()
        copy = pltpu.make_async_remote_copy(
            region, region, self.send.take(), recv, device_id=self.to[way], device_id_type=MESH
        )
        copy.start()
        self.sent.append(copy)
        return pltpu.make_async_remote_copy(
            lands, lands, self.send.sems.at[0], recv, device_id=self.to[way], device_id_type=MESH
        )

    def push(self, way, dx, dy, part):
        wx, wy = self.WAYS[way]
        there = ((dx - wx) % NX, (dy - wy) % NY)
        region = self.buf.at[self.chip(dx, dy) + (self.c,) + part]
        lands = self.buf.at[self.chip(*there) + (self.c,) + part]
        self.landing[(there, part)] = self.move(way, region, lands)

    def arrive(self, dx, dy, part):
        self.landing.pop(((dx % NX, dy % NY), part)).wait_recv()

    def share(self, dx, dy):
        region = self.buf.at[self.chip(dx, dy) + (self.c,)]
        lands = self.buf.at[self.chip(dx, dy) + (1 - self.c,)]
        self.partner[(dx % NX, dy % NY)] = self.move("core", region, lands)

    def whole(self, dx, dy):
        self.partner.pop((dx % NX, dy % NY)).wait_recv()

    def start(self):
        for first, second in ((0, 1), (1, 0)):
            for way in ("x2", "+x", "-x"):
                self.push(way, 0, 0, (first,))
            for way in ("y2", "+y", "-y"):
                self.push(way, 0, 0, (second,))
        self.share(0, 0)

    def onward(self, places):
        for dx, dy in places:
            part = (0,) if dx else (1,)
            self.arrive(dx, dy, part)
            for side in ("y2", "+y", "-y") if dx else ("x2", "+x", "-x"):
                self.push(side, dx, dy, part)

    def fill(self, places):
        for dx, dy in places:
            self.arrive(dx, dy, (1,) if dx else (0,))
            self.share(dx, dy)

    def corners(self, places):
        for dx, dy in places:
            self.arrive(dx, dy, (0,))
            self.arrive(dx, dy, (1,))
            self.share(dx, dy)

    def wave(self, number):
        if number == 1:
            self.start()
        elif number == 2:
            self.onward(self.NEAR)
        elif number == 3:
            self.onward(self.AXES)
            self.fill(self.NEAR + self.AXES)
        elif number == 4:
            self.corners(self.CORNERS[:4])
        elif number == 5:
            self.corners(self.CORNERS[4:])
        else:
            for dx, dy in list(self.partner):
                self.whole(dx, dy)

    def drain(self):
        for copy in self.sent:
            copy.wait_send()


class Ring:
    def __init__(self, n, z, t, held, full, got, owner, flows, send, recv, landed):
        self.n, self.z, self.t, self.held, self.full, self.got = n, z, t, held, full, got
        self.owner, self.flows, self.landed = owner, flows, landed
        self.most = max(hops for _, _, hops in flows)
        self.base = [sum(h for _, _, h in flows[:i]) for i in range(len(flows))]
        self.recv = [[[recv.take() for _ in range(SUBS)] for _ in range(2 * h)] for _, _, h in flows]
        self.send = [[[send.take() for _ in range(SUBS)] for _ in range(2 * h)] for _, _, h in flows]
        self.sent = []
        self.ready = []

    def wrap(self, p):
        return lax.rem(p + 4 * self.n, self.n)

    def copy(self, f, step, sub, src, dst):
        sign, base, hops = self.flows[f]
        away = base + 1 if step in (hops - 1, hops) else 1
        return pltpu.make_async_remote_copy(
            src,
            dst,
            self.send[f][step][sub],
            self.recv[f][step][sub],
            device_id=(self.wrap(self.z + sign * away), self.t),
            device_id_type=MESH,
        )

    def go(self, f, step, sub, src, dst):
        copy = self.copy(f, step, sub, src, dst)
        copy.start()
        self.sent.append(copy)

    def came(self, f, step, sub, where):
        self.copy(f, step, sub, where, where).wait_recv()

    def slot(self, f, step, sub):
        return self.got.at[self.base[f] + step, sub]

    def spread(self, f, j):
        sign, base, _ = self.flows[f]
        return self.wrap(self.z - sign * (base + 1 + j))

    def combine(self, sub):
        back = self.z - self.owner
        back = jnp.where(back < 0, back + self.n, back)
        best = self.held[self.z, sub]
        for f, (sign, base, hops) in enumerate(self.flows):
            slot = self.slot(f, hops - 1, sub)
            self.came(f, hops - 1, sub, slot)
            far = back if sign > 0 else self.n - back
            best = jnp.where(jnp.logical_and(far > base, far <= base + hops), slot[...], best)
        here = self.full.at[self.z, sub]
        here[...] = best
        for f, (_, _, hops) in enumerate(self.flows):
            self.go(f, hops, sub, here, here)

    def step(self, k):
        mine = self.owner == self.z
        flows = sorted(range(len(self.flows)), key=lambda f: -self.flows[f][1])
        for sub in range(SUBS):
            if k == self.most:
                self.combine(sub)
            for f in flows:
                sign, base, hops = self.flows[f]
                if k < hops:
                    src = self.held.at[self.wrap(self.z + sign * (base + hops - k)), sub]
                    if k > 0:
                        slot = self.slot(f, k - 1, sub)
                        self.came(f, k - 1, sub, slot)
                        slot[...] = jnp.where(mine, src[...], slot[...])
                        src = slot
                    self.go(f, k, sub, src, self.slot(f, k, sub))
                j = k - self.most - 1
                if 0 <= j < hops:
                    block = self.full.at[self.spread(f, j), sub]
                    self.came(f, hops + j, sub, block)
                    if j + 1 < hops:
                        self.go(f, hops + j + 1, sub, block, block)
        if k == self.most:
            self.ready.append(self.z)
        for f, (_, _, hops) in enumerate(self.flows):
            if 0 <= k - self.most - 1 < hops:
                self.ready.append(self.spread(f, k - self.most - 1))

    def flush(self):
        for p in self.ready:
            self.landed(p)
        self.ready = []

    def drain(self):
        for copy in self.sent:
            copy.wait_send()


def body(
    n_dp,
    owners,
    acts,
    grads,
    held_in_hbm,
    held_out_hbm,
    eig_hbm,
    out_hbm,
    all_acts,
    all_grads,
    all_rot,
    held_in,
    held_out,
    full_in,
    full_out,
    got_in,
    got_out,
    sum_in,
    sum_out,
    eig,
    scale,
    out,
    send_sems,
    recv_sems,
    load_sems,
):
    z = lax.axis_index("dp")
    t = lax.axis_index("tensor")
    c = lax.rem(t, 2)
    x = lax.rem(lax.div(t, 2), NX)
    y = lax.div(t, 2 * NX)

    def chip(yy, xx, cc):
        return (z, (lax.rem(yy + NY, NY) * NX + lax.rem(xx + NX, NX)) * 2 + cc)

    to = {
        "+x": chip(y, x + 1, c),
        "-x": chip(y, x - 1, c),
        "+y": chip(y + 1, x, c),
        "-y": chip(y - 1, x, c),
        "x2": chip(y, x + 2, c),
        "y2": chip(y + 2, x, c),
        "core": chip(y, x, 1 - c),
    }
    in_flows = ((1, 0, 2), (1, 2, 6), (-1, 0, 2), (-1, 2, 5))
    out_flows = ((1, 0, 8), (-1, 0, 7))
    reach = sorted({sign * (base + 1) for sign, base, _ in in_flows + out_flows})

    loads = [
        pltpu.make_async_copy(held_in_hbm, held_in, load_sems.at[0]),
        pltpu.make_async_copy(acts, all_acts.at[y, x, c], load_sems.at[1]),
        pltpu.make_async_copy(held_out_hbm, held_out, load_sems.at[2]),
        pltpu.make_async_copy(grads, all_grads.at[y, x, c], load_sems.at[3]),
        pltpu.make_async_copy(eig_hbm, eig, load_sems.at[4]),
    ]
    for load in loads:
        load.start()

    barrier = pltpu.get_barrier_semaphore()
    around = list(to.values()) + [(lax.rem(z + n_dp + far, n_dp), t) for far in sorted(reach + [-far for far in reach if -far not in reach])]
    for device in around:
        pl.semaphore_signal(barrier, inc=1, device_id=device, device_id_type=MESH)
    pl.semaphore_wait(barrier, len(around))

    send, recv = Slots(send_sems), Slots(recv_sems)
    acts_plane = Plane(all_acts, (y, x, c), to, send, recv)
    grads_plane = Plane(all_grads, (y, x, c), to, send, recv)
    rot_plane = Plane(all_rot, (y, x, c), to, send, recv)
    chunk = lambda ref, p, core: ref[lax.div(p, NX), lax.rem(p, NX), core].reshape(-1, ref.shape[-1])

    def add_to(total, ref, full):
        def landed(p):
            left = jnp.concatenate([chunk(ref, p, 0), chunk(ref, p, 1)], axis=1)
            right = full[p].reshape(-1, full.shape[-1])
            total[...] += jnp.dot(left, right, preferred_element_type=jnp.float32)

        return landed

    ring_in = Ring(
        n_dp, z, t, held_in, full_in, got_in, owners[0, t], in_flows, send, recv, add_to(sum_in, all_acts, full_in)
    )
    ring_out = Ring(
        n_dp, z, t, held_out, full_out, got_out, owners[1, t], out_flows, send, recv, add_to(sum_out, all_grads, full_out)
    )
    for load in loads:
        load.wait()
    done = set()
    for word in " ".join(ORDER).split():
        kind, number = word[0], int(word[1:])
        if kind == "i":
            ring_in.step(number)
        elif kind == "o":
            ring_out.step(number)
        elif kind == "a":
            acts_plane.wave(number)
        elif kind == "g":
            grads_plane.wave(number)
        elif kind == "r":
            if number == 1:
                rot = sum_in[...].astype(jnp.bfloat16)
                all_rot.at[y, x, c][...] = rot.reshape(all_rot.shape[3:])
            rot_plane.wave(number)
        elif kind == "e":
            scale[...] = 1.0 / (eig[...].astype(jnp.float32) + damping)
            sum_in[...] = jnp.zeros_like(sum_in)
            sum_out[...] = jnp.zeros_like(sum_out)
        else:
            turned = jnp.transpose(sum_out[...]).astype(jnp.bfloat16)
        done.add(word)
        if "a6" in done:
            ring_in.flush()
        if "g6" in done:
            ring_out.flush()

    tokens = sum_in.shape[0]
    stores = []
    for i, (dx, dy) in enumerate(((0, 0),) + Plane.NEAR + Plane.AXES + Plane.CORNERS):
        rot_plane.whole(dx, dy)
        p = lax.rem(y + (dy % NY), NY) * NX + lax.rem(x + (dx % NX), NX)
        right = jnp.concatenate([chunk(all_rot, p, 0), chunk(all_rot, p, 1)], axis=1)
        cols = pl.ds(pl.multiple_of(p * right.shape[1], right.shape[1]), right.shape[1])
        product = jnp.dot(turned, right, preferred_element_type=jnp.float32) * (1.0 / tokens)
        out[:, cols] = (product * scale[:, cols]).astype(jnp.bfloat16)
        stores.append(pltpu.make_async_copy(out.at[:, cols], out_hbm.at[:, cols], load_sems.at[5 + i]))
        stores[-1].start()
    for user in (acts_plane, grads_plane, rot_plane, ring_in, ring_out):
        user.drain()
    for store in stores:
        store.wait()


def shards(n_dp, acts, grads, basis_in_held, basis_out_held, owners, eig_lambda):
    tok, width = acts.shape[1:]
    depth = basis_in_held.shape[1]
    rows = depth // n_dp // SUBS
    slice_shape = (2, tok // 2, width)
    held_shape = (n_dp, SUBS, rows, width)
    any_space = pl.BlockSpec(memory_space=pl.ANY)
    bf16, f32 = jnp.bfloat16, jnp.float32
    out = pl.pallas_call(
        functools.partial(body, n_dp),
        out_shape=jax.ShapeDtypeStruct(eig_lambda.shape, bf16),
        in_specs=[pl.BlockSpec(memory_space=pltpu.SMEM)] + [any_space] * 5,
        out_specs=any_space,
        scratch_shapes=[
            pltpu.VMEM((NY, NX, 2) + slice_shape, bf16),
            pltpu.VMEM((NY, NX, 2) + slice_shape, bf16),
            pltpu.VMEM((NY, NX, 2) + slice_shape, bf16),
            pltpu.VMEM(held_shape, bf16),
            pltpu.VMEM(held_shape, bf16),
            pltpu.VMEM(held_shape, bf16),
            pltpu.VMEM(held_shape, bf16),
            pltpu.VMEM((n_dp - 1,) + held_shape[1:], bf16),
            pltpu.VMEM((n_dp - 1,) + held_shape[1:], bf16),
            pltpu.VMEM((tok, width), f32),
            pltpu.VMEM((tok, width), f32),
            pltpu.VMEM(eig_lambda.shape, bf16),
            pltpu.VMEM(eig_lambda.shape, f32),
            pltpu.VMEM(eig_lambda.shape, bf16),
            pltpu.SemaphoreType.DMA((138 + 4 * (n_dp - 1) * SUBS,)),
            pltpu.SemaphoreType.DMA((138 + 4 * (n_dp - 1) * SUBS,)),
            pltpu.SemaphoreType.DMA((5 + NX * NY,)),
        ],
        compiler_params=pltpu.CompilerParams(
            collective_id=0, has_side_effects=True, vmem_limit_bytes=56 * 1024 * 1024
        ),
    )(
        owners,
        acts[0].reshape(slice_shape),
        grads[0].reshape(slice_shape),
        basis_in_held[0].reshape(held_shape),
        basis_out_held[0].reshape(held_shape),
        eig_lambda,
    )
    return out[None]


def solution(mesh):
    placed = (
        P("dp", None, "tensor"),
        P("dp", None, "tensor"),
        P("dp", None, "tensor"),
        P("dp", None, "tensor"),
        P(),
        P("tensor", None),
    )
    return jax.shard_map(
        functools.partial(shards, mesh.shape["dp"]),
        mesh=mesh,
        in_specs=placed,
        out_specs=P("dp", "tensor", None),
        check_vma=False,
    )
```

```python
import functools

import jax
import jax.numpy as jnp
from jax import lax
from jax.experimental import pallas as pl
from jax.experimental.pallas import tpu as pltpu
from jax.sharding import PartitionSpec as P

damping = 0.01
MESH = pl.DeviceIdType.MESH
NX = 4
NY = 4
SUBS = 2
ORDER = (
    "i0 o0 a1 e0", "i1 o1 i2 o2", "a2 i3 o3 i4", "o4 a3 i5 o5", "a4 i6 o6 a5", "a6 g1 i7 o7",
    "i8 o8 g2 i9", "o9 i10 o10 g3", "i11 o11 g4 i12", "o12 r1 g5 g6", "o13 r2 o14 r3", "o15 r4 o16 t0",
    "r5",
)


class Slots:
    def __init__(self, sems):
        self.sems = sems
        self.used = 0

    def take(self):
        self.used += 1
        return self.sems.at[self.used - 1]


class Plane:
    WAYS = {"x2": (2, 0), "+x": (1, 0), "-x": (-1, 0), "y2": (0, 2), "+y": (0, 1), "-y": (0, -1)}
    NEAR = ((-1, 0), (1, 0), (0, -1), (0, 1))
    AXES = ((2, 0), (0, 2))
    CORNERS = ((-1, -1), (1, -1), (-1, 1), (1, 1), (-1, 2), (1, 2), (2, -1), (2, 1), (2, 2))

    def __init__(self, buf, where, to, send, recv):
        self.buf, self.to, self.send, self.recv = buf, to, send, recv
        self.y, self.x, self.c = where
        self.landing = {}
        self.partner = {}
        self.sent = []

    def chip(self, dx, dy):
        return lax.rem(self.y + (dy % NY), NY), lax.rem(self.x + (dx % NX), NX)

    def move(self, way, region, lands):
        recv = self.recv.take()
        copy = pltpu.make_async_remote_copy(
            region, region, self.send.take(), recv, device_id=self.to[way], device_id_type=MESH
        )
        copy.start()
        self.sent.append(copy)
        return pltpu.make_async_remote_copy(
            lands, lands, self.send.sems.at[0], recv, device_id=self.to[way], device_id_type=MESH
        )

    def push(self, way, dx, dy, part):
        wx, wy = self.WAYS[way]
        there = ((dx - wx) % NX, (dy - wy) % NY)
        region = self.buf.at[self.chip(dx, dy) + (self.c,) + part]
        lands = self.buf.at[self.chip(*there) + (self.c,) + part]
        self.landing[(there, part)] = self.move(way, region, lands)

    def arrive(self, dx, dy, part):
        self.landing.pop(((dx % NX, dy % NY), part)).wait_recv()

    def share(self, dx, dy):
        region = self.buf.at[self.chip(dx, dy) + (self.c,)]
        lands = self.buf.at[self.chip(dx, dy) + (1 - self.c,)]
        self.partner[(dx % NX, dy % NY)] = self.move("core", region, lands)

    def whole(self, dx, dy):
        self.partner.pop((dx % NX, dy % NY)).wait_recv()

    def start(self):
        for first, second in ((0, 1), (1, 0)):
            for way in ("x2", "+x", "-x"):
                self.push(way, 0, 0, (first,))
            for way in ("y2", "+y", "-y"):
                self.push(way, 0, 0, (second,))
        self.share(0, 0)

    def onward(self, places):
        for dx, dy in places:
            part = (0,) if dx else (1,)
            self.arrive(dx, dy, part)
            for side in ("y2", "+y", "-y") if dx else ("x2", "+x", "-x"):
                self.push(side, dx, dy, part)

    def fill(self, places):
        for dx, dy in places:
            self.arrive(dx, dy, (1,) if dx else (0,))
            self.share(dx, dy)

    def corners(self, places):
        for dx, dy in places:
            self.arrive(dx, dy, (0,))
            self.arrive(dx, dy, (1,))
            self.share(dx, dy)

    def wave(self, number):
        if number == 1:
            self.start()
        elif number == 2:
            self.onward(self.NEAR)
        elif number == 3:
            self.onward(self.AXES)
            self.fill(self.NEAR + self.AXES)
        elif number == 4:
            self.corners(self.CORNERS[:4])
        elif number == 5:
            self.corners(self.CORNERS[4:])
        else:
            for dx, dy in list(self.partner):
                self.whole(dx, dy)

    def drain(self):
        for copy in self.sent:
            copy.wait_send()


class Ring:
    def __init__(self, n, z, t, held, full, got, owner, flows, send, recv, landed):
        self.n, self.z, self.t, self.held, self.full, self.got = n, z, t, held, full, got
        self.owner, self.flows, self.landed = owner, flows, landed
        self.most = max(hops for _, _, hops in flows)
        self.base = [sum(h for _, _, h in flows[:i]) for i in range(len(flows))]
        self.recv = [[[recv.take() for _ in range(SUBS)] for _ in range(2 * h)] for _, _, h in flows]
        self.send = [[[send.take() for _ in range(SUBS)] for _ in range(2 * h)] for _, _, h in flows]
        self.sent = []
        self.ready = []

    def wrap(self, p):
        return lax.rem(p + 4 * self.n, self.n)

    def copy(self, f, step, sub, src, dst):
        sign, base, hops = self.flows[f]
        away = base + 1 if step in (hops - 1, hops) else 1
        return pltpu.make_async_remote_copy(
            src,
            dst,
            self.send[f][step][sub],
            self.recv[f][step][sub],
            device_id=(self.wrap(self.z + sign * away), self.t),
            device_id_type=MESH,
        )

    def go(self, f, step, sub, src, dst):
        copy = self.copy(f, step, sub, src, dst)
        copy.start()
        self.sent.append(copy)

    def came(self, f, step, sub, where):
        self.copy(f, step, sub, where, where).wait_recv()

    def slot(self, f, step, sub):
        return self.got.at[self.base[f] + step, sub]

    def spread(self, f, j):
        sign, base, _ = self.flows[f]
        return self.wrap(self.z - sign * (base + 1 + j))

    def combine(self, sub):
        back = self.z - self.owner
        back = jnp.where(back < 0, back + self.n, back)
        best = self.held[self.z, sub]
        for f, (sign, base, hops) in enumerate(self.flows):
            slot = self.slot(f, hops - 1, sub)
            self.came(f, hops - 1, sub, slot)
            far = back if sign > 0 else self.n - back
            best = jnp.where(jnp.logical_and(far > base, far <= base + hops), slot[...], best)
        here = self.full.at[self.z, sub]
        here[...] = best
        for f, (_, _, hops) in enumerate(self.flows):
            self.go(f, hops, sub, here, here)

    def step(self, k):
        mine = self.owner == self.z
        flows = sorted(range(len(self.flows)), key=lambda f: -self.flows[f][1])
        for sub in range(SUBS):
            if k == self.most:
                self.combine(sub)
            for f in flows:
                sign, base, hops = self.flows[f]
                if k < hops:
                    src = self.held.at[self.wrap(self.z + sign * (base + hops - k)), sub]
                    if k > 0:
                        slot = self.slot(f, k - 1, sub)
                        self.came(f, k - 1, sub, slot)
                        slot[...] = jnp.where(mine, src[...], slot[...])
                        src = slot
                    self.go(f, k, sub, src, self.slot(f, k, sub))
                j = k - self.most - 1
                if 0 <= j < hops:
                    block = self.full.at[self.spread(f, j), sub]
                    self.came(f, hops + j, sub, block)
                    if j + 1 < hops:
                        self.go(f, hops + j + 1, sub, block, block)
        if k == self.most:
            self.ready.append(self.z)
        for f, (_, _, hops) in enumerate(self.flows):
            if 0 <= k - self.most - 1 < hops:
                self.ready.append(self.spread(f, k - self.most - 1))

    def flush(self):
        for p in self.ready:
            self.landed(p)
        self.ready = []

    def drain(self):
        for copy in self.sent:
            copy.wait_send()


def body(
    n_dp,
    owners,
    acts,
    grads,
    held_in_hbm,
    held_out_hbm,
    eig_hbm,
    out_hbm,
    all_acts,
    all_grads,
    all_rot,
    held_in,
    held_out,
    full_in,
    full_out,
    got_in,
    got_out,
    sum_in,
    sum_out,
    eig,
    scale,
    out,
    send_sems,
    recv_sems,
    load_sems,
):
    z = lax.axis_index("dp")
    t = lax.axis_index("tensor")
    c = lax.rem(t, 2)
    x = lax.rem(lax.div(t, 2), NX)
    y = lax.div(t, 2 * NX)

    def chip(yy, xx, cc):
        return (z, (lax.rem(yy + NY, NY) * NX + lax.rem(xx + NX, NX)) * 2 + cc)

    to = {
        "+x": chip(y, x + 1, c),
        "-x": chip(y, x - 1, c),
        "+y": chip(y + 1, x, c),
        "-y": chip(y - 1, x, c),
        "x2": chip(y, x + 2, c),
        "y2": chip(y + 2, x, c),
        "core": chip(y, x, 1 - c),
    }
    in_flows = ((1, 0, 2), (1, 2, 6), (-1, 0, 2), (-1, 2, 5))
    out_flows = ((1, 0, 8), (-1, 0, 7))
    reach = sorted({sign * (base + 1) for sign, base, _ in in_flows + out_flows})

    loads = [
        pltpu.make_async_copy(held_in_hbm, held_in, load_sems.at[0]),
        pltpu.make_async_copy(acts, all_acts.at[y, x, c], load_sems.at[1]),
        pltpu.make_async_copy(held_out_hbm, held_out, load_sems.at[2]),
        pltpu.make_async_copy(grads, all_grads.at[y, x, c], load_sems.at[3]),
        pltpu.make_async_copy(eig_hbm, eig, load_sems.at[4]),
    ]
    for load in loads:
        load.start()

    barrier = pltpu.get_barrier_semaphore()
    around = list(to.values()) + [(lax.rem(z + n_dp + far, n_dp), t) for far in sorted(reach + [-far for far in reach if -far not in reach])]
    for device in around:
        pl.semaphore_signal(barrier, inc=1, device_id=device, device_id_type=MESH)
    pl.semaphore_wait(barrier, len(around))

    send, recv = Slots(send_sems), Slots(recv_sems)
    acts_plane = Plane(all_acts, (y, x, c), to, send, recv)
    grads_plane = Plane(all_grads, (y, x, c), to, send, recv)
    rot_plane = Plane(all_rot, (y, x, c), to, send, recv)
    chunk = lambda ref, p, core: ref[lax.div(p, NX), lax.rem(p, NX), core].reshape(-1, ref.shape[-1])

    def add_to(total, ref, full):
        def landed(p):
            left = jnp.concatenate([chunk(ref, p, 0), chunk(ref, p, 1)], axis=1)
            right = full[p].reshape(-1, full.shape[-1])
            total[...] += jnp.dot(left, right, preferred_element_type=jnp.float32)

        return landed

    ring_in = Ring(
        n_dp, z, t, held_in, full_in, got_in, owners[0, t], in_flows, send, recv, add_to(sum_in, all_acts, full_in)
    )
    ring_out = Ring(
        n_dp, z, t, held_out, full_out, got_out, owners[1, t], out_flows, send, recv, add_to(sum_out, all_grads, full_out)
    )
    for load in loads:
        load.wait()
    done = set()
    for word in " ".join(ORDER).split():
        kind, number = word[0], int(word[1:])
        if kind == "i":
            ring_in.step(number)
        elif kind == "o":
            ring_out.step(number)
        elif kind == "a":
            acts_plane.wave(number)
        elif kind == "g":
            grads_plane.wave(number)
        elif kind == "r":
            if number == 1:
                rot = sum_in[...].astype(jnp.bfloat16)
                all_rot.at[y, x, c][...] = rot.reshape(all_rot.shape[3:])
            rot_plane.wave(number)
        elif kind == "e":
            scale[...] = 1.0 / (eig[...].astype(jnp.float32) + damping)
            sum_in[...] = jnp.zeros_like(sum_in)
            sum_out[...] = jnp.zeros_like(sum_out)
        else:
            turned = jnp.transpose(sum_out[...]).astype(jnp.bfloat16)
            for user in (acts_plane, grads_plane, ring_in, ring_out):
                user.drain()
        done.add(word)
        if "a6" in done:
            ring_in.flush()
        if "g6" in done:
            ring_out.flush()

    tokens = sum_in.shape[0]
    stores = []
    for i, (dx, dy) in enumerate(((0, 0),) + Plane.NEAR + Plane.AXES + Plane.CORNERS):
        rot_plane.whole(dx, dy)
        p = lax.rem(y + (dy % NY), NY) * NX + lax.rem(x + (dx % NX), NX)
        right = jnp.concatenate([chunk(all_rot, p, 0), chunk(all_rot, p, 1)], axis=1)
        cols = pl.ds(pl.multiple_of(p * right.shape[1], right.shape[1]), right.shape[1])
        product = jnp.dot(turned, right, preferred_element_type=jnp.float32) * (1.0 / tokens)
        out[:, cols] = (product * scale[:, cols]).astype(jnp.bfloat16)
        stores.append(pltpu.make_async_copy(out.at[:, cols], out_hbm.at[:, cols], load_sems.at[5 + i]))
        stores[-1].start()
    rot_plane.drain()
    for store in stores:
        store.wait()


def shards(n_dp, acts, grads, basis_in_held, basis_out_held, owners, eig_lambda):
    tok, width = acts.shape[1:]
    depth = basis_in_held.shape[1]
    rows = depth // n_dp // SUBS
    slice_shape = (2, tok // 2, width)
    held_shape = (n_dp, SUBS, rows, width)
    any_space = pl.BlockSpec(memory_space=pl.ANY)
    bf16, f32 = jnp.bfloat16, jnp.float32
    out = pl.pallas_call(
        functools.partial(body, n_dp),
        out_shape=jax.ShapeDtypeStruct(eig_lambda.shape, bf16),
        in_specs=[pl.BlockSpec(memory_space=pltpu.SMEM)] + [any_space] * 5,
        out_specs=any_space,
        scratch_shapes=[
            pltpu.VMEM((NY, NX, 2) + slice_shape, bf16),
            pltpu.VMEM((NY, NX, 2) + slice_shape, bf16),
            pltpu.VMEM((NY, NX, 2) + slice_shape, bf16),
            pltpu.VMEM(held_shape, bf16),
            pltpu.VMEM(held_shape, bf16),
            pltpu.VMEM(held_shape, bf16),
            pltpu.VMEM(held_shape, bf16),
            pltpu.VMEM((n_dp - 1,) + held_shape[1:], bf16),
            pltpu.VMEM((n_dp - 1,) + held_shape[1:], bf16),
            pltpu.VMEM((tok, width), f32),
            pltpu.VMEM((tok, width), f32),
            pltpu.VMEM(eig_lambda.shape, bf16),
            pltpu.VMEM(eig_lambda.shape, f32),
            pltpu.VMEM(eig_lambda.shape, bf16),
            pltpu.SemaphoreType.DMA((138 + 4 * (n_dp - 1) * SUBS,)),
            pltpu.SemaphoreType.DMA((138 + 4 * (n_dp - 1) * SUBS,)),
            pltpu.SemaphoreType.DMA((5 + NX * NY,)),
        ],
        compiler_params=pltpu.CompilerParams(
            collective_id=0, has_side_effects=True, vmem_limit_bytes=56 * 1024 * 1024
        ),
    )(
        owners,
        acts[0].reshape(slice_shape),
        grads[0].reshape(slice_shape),
        basis_in_held[0].reshape(held_shape),
        basis_out_held[0].reshape(held_shape),
        eig_lambda,
    )
    return out[None]


def solution(mesh):
    placed = (
        P("dp", None, "tensor"),
        P("dp", None, "tensor"),
        P("dp", None, "tensor"),
        P("dp", None, "tensor"),
        P(),
        P("tensor", None),
    )
    return jax.shard_map(
        functools.partial(shards, mesh.shape["dp"]),
        mesh=mesh,
        in_specs=placed,
        out_specs=P("dp", "tensor", None),
        check_vma=False,
    )
```
